256 devices in a mesh: fsdp: 256 (over z, x, y, core).
Axes of the slice: x: 4, y: 4, z: 8, core: 2. Of those that a mesh axis runs over, the one named last changes fastest.
Arguments:
- inputs: bfloat16 [256, 4096], P('fsdp'), may hold values from -6 to 6
- norm_gain: bfloat16 [4096], replicated, may hold values from 0.099609375 to 1.8984375
- lengths: int32 [2], replicated, may hold values from 1 to 128, 192 in all
- gate_rows: bfloat16 [10240, 4096], P('fsdp'), may hold values from -0.09375 to 0.09375
- up_rows: bfloat16 [10240, 4096], P('fsdp'), may hold values from -0.09375 to 0.09375
- down_rows: bfloat16 [10240, 4096], P('fsdp'), may hold values from -0.25 to 0.25
- krylov_gate: bfloat16 [8, 10240, 4096], P(None, 'fsdp'), may hold values from -30 to 30
- krylov_up: bfloat16 [8, 10240, 4096], P(None, 'fsdp'), may hold values from -30 to 30
- krylov_down: bfloat16 [8, 10240, 4096], P(None, 'fsdp'), may hold values from -30 to 30
Outputs:
- new_gate: bfloat16 [10240, 4096], P('fsdp')
- new_up: bfloat16 [10240, 4096], P('fsdp')
- new_down: bfloat16 [10240, 4096], P('fsdp')
- coefficients: float32 [9], replicated
The draws below stay inside these ranges and needn't reach their ends.
Inputs may be any that keep to these rules, and one draw needn't show every extreme that they name: The lengths sum to exactly 192.
All inputs are finite; a program needn't handle non-finite values.
Results may differ from the reference program's by a relative error of at most 0.0051.
The reference program's roundings to bfloat16 on the way (of `normed`, `probe_gate`, `hidden`, `tangent`, `loss_t` and `s_term`) count: a program that leaves them out, or rounds other values in their place, can miss the bound.
Values may be sent and summed in bfloat16 or wider, within the bound.
A program may use at most 64 MiB of HBM per device.

```python
import math
import jax
import jax.numpy as jnp
import numpy as np
from jax import lax

D = 4096
FF = 10240
BASIS = 8
LEN = 128
SEQS = 2
TOKENS = 256
LIVE = 192


def krylov_common(key, salt):
    key = jax.random.fold_in(key, salt)
    keys = jax.random.split(key, 3)
    ramp = jnp.exp(math.log(3.0) * jnp.arange(FF, dtype=jnp.float32) / FF)
    row_scale = jnp.exp(jax.random.uniform(keys[0], (1, FF, 1), jnp.float32, math.log(0.4), math.log(4.0)))
    shared = jax.random.normal(keys[1], (1, FF, D), jnp.float32)
    own = jax.random.normal(keys[2], (BASIS, FF, D), jnp.float32)
    col_scale = jnp.ones((1, 1, D), jnp.float32)
    mixed = 0.6 * shared + 0.8 * own
    values = ramp[None, :, None] * row_scale * col_scale * mixed
    return jnp.clip(values, -30.0, 30.0).astype(jnp.bfloat16)


def draw_krylov_gate(key, part):
    return krylov_common(key, 11)


def draw_krylov_up(key, part):
    return krylov_common(key, 12)


def draw_krylov_down(key, part):
    return krylov_common(key, 13)


def spiked(array, key, source, target, blocks, factor):
    owner, partner = [(jnp.arange(array.shape[position]) // (array.shape[position] // blocks)).reshape([-1 if axis == position else 1 for axis in range(array.ndim)]) for position in (source, target)]
    chosen = jax.random.permutation(key, blocks)[partner]
    strong = (owner == chosen) | (owner == (partner + blocks // 2) % blocks)
    return jnp.where(strong, factor * array, array)


def block_scale(stream_key, shape, pieces, low, top_value):
    loudness = 1.0
    for axis_at, blocks in pieces:
        steps = jax.random.uniform(jax.random.fold_in(jax.random.fold_in(stream_key, 6), axis_at), (blocks,), jnp.float32, low / len(pieces), top_value / len(pieces))
        loudness = loudness * jnp.repeat(jnp.exp(steps), shape[axis_at] // blocks).reshape((-1,) + (1,) * (len(shape) - 1 - axis_at))
    return loudness


def profile(count, total, reach, lean):
    loads = [(1 << 20) // math.isqrt(rank ** lean) + 1 for rank in range(2, count + 1)]
    rest, counts = total - reach - (count - 1), [1] * (count - 1)
    while rest > 0:
        movable = [i for i in range(count - 1) if counts[i] < reach]
        whole, remaining = sum([loads[i] for i in movable]), rest
        for i in movable:
            more = min(reach - counts[i], max(1, remaining * loads[i] // whole), rest)
            counts[i] = counts[i] + more
            rest = rest - more
    return np.array([reach] + counts)


def uneven(stream_key, amount, total, bound, skew):
    if amount == 2:
        one = jax.random.randint(stream_key, (), max(1, total - bound), min(bound, total - 1) + 1)
        return jnp.stack([one, total - one])
    sizes = jnp.asarray(profile(amount, total, bound, skew), jnp.int32)
    couples = (amount - 1) // 2
    giver, receiver = sizes[1:1 + 2 * couples:2], sizes[2:2 + 2 * couples:2]
    slack = jnp.minimum(giver - 1, bound - receiver)
    passed = jax.random.randint(jax.random.fold_in(stream_key, 1), (couples,), 0, 1 << 20) % (slack + 1)
    sizes = sizes.at[1:1 + 2 * couples:2].set(giver - passed).at[2:2 + 2 * couples:2].set(receiver + passed)
    return sizes[jax.random.permutation(jax.random.fold_in(stream_key, 2), amount)]


def bell_draw(rng, shape, deviation, bound, shards=(), kind=jnp.bfloat16):
    level = block_scale(rng, shape, shards, -0.22, 0.18) if shards else 1.0
    entries = jax.random.normal(rng, shape, jnp.float32) * deviation * level
    return jnp.minimum(jnp.maximum(entries, -bound), bound).astype(kind)


def noise_with(own_key, shape, deviation, limit, cuts, heavy, held_as=jnp.bfloat16):
    values = deviation * jax.random.normal(own_key, shape, jnp.float32)
    if cuts:
        values = values * block_scale(own_key, shape, cuts, -0.22, 0.18)
    return jnp.clip(spiked(values, jax.random.fold_in(own_key, 3), *heavy), -limit, limit).astype(held_as)


def setup_inputs(seed: int = 0) -> dict:
    key_of = jax.random.split(jax.random.key(seed), 10)
    inputs = bell_draw(key_of[0], (TOKENS, D), 1.0, 6.0, ((0, 256),))
    norm_gain = jnp.clip(1.0 + 0.18 * jax.random.normal(key_of[1], (D,), jnp.float32), 0.099609375, 1.8984375).astype(jnp.bfloat16)
    lengths = uneven(key_of[2], SEQS, LIVE, LEN, 0).astype(jnp.int32)
    gate_rows = bell_draw(key_of[3], (FF, D), D ** -0.5, 0.09375, ((0, 256),))
    up_rows = bell_draw(key_of[4], (FF, D), D ** -0.5, 0.09375, ((0, 256),))
    down_rows = noise_with(key_of[5], (FF, D), FF ** -0.5, 0.25, ((0, 256),), (0, 1, 256, 6.0))
    krylov_gate = draw_krylov_gate(jax.random.fold_in(key_of[9], 71), 0)
    krylov_up = draw_krylov_up(jax.random.fold_in(key_of[9], 71), 0)
    krylov_down = draw_krylov_down(jax.random.fold_in(key_of[9], 71), 0)
    return {"inputs": inputs, "norm_gain": norm_gain, "lengths": lengths, "gate_rows": gate_rows, "up_rows": up_rows, "down_rows": down_rows, "krylov_gate": krylov_gate, "krylov_up": krylov_up, "krylov_down": krylov_down}


def gelu_pair(gate_pre):
    coef = math.sqrt(2.0 / math.pi)
    cube = gate_pre * gate_pre * gate_pre
    tanh_val = jnp.tanh(coef * (gate_pre + 0.044715 * cube))
    act = 0.5 * gate_pre * (1.0 + tanh_val)
    slope = 0.5 * (1.0 + tanh_val) + 0.5 * gate_pre * (1.0 - tanh_val * tanh_val) * coef * (1.0 + 3.0 * 0.044715 * gate_pre * gate_pre)
    return (act, slope)

def contract_first(left, right):
    return lax.dot_general(left, right, (((0,), (0,)), ((), ())), preferred_element_type=jnp.float32)

def contract_last(left, right):
    return lax.dot_general(left, right, (((1,), (1,)), ((), ())), preferred_element_type=jnp.float32)

def reference(inputs, norm_gain, lengths, gate_rows, up_rows, down_rows, krylov_gate, krylov_up, krylov_down):
    wide = inputs.astype(jnp.float32)
    normed = (wide * lax.rsqrt(lax.optimization_barrier(jnp.mean(wide * wide, axis=1, keepdims=True)) + 1e-06) * norm_gain.astype(jnp.float32)).astype(jnp.bfloat16)
    inv_d = 1.0 / math.sqrt(D)
    inv_ff = 1.0 / math.sqrt(FF)
    probe_gate = krylov_gate[BASIS - 1]
    probe_up = krylov_up[BASIS - 1]
    probe_down = krylov_down[BASIS - 1]
    gate_pre = contract_last(gate_rows, normed)
    up_pre = contract_last(up_rows, normed)
    tan_gate = contract_last(probe_gate, normed) * inv_d
    tan_up = contract_last(probe_up, normed) * inv_d
    act, slope = gelu_pair(gate_pre)
    hidden = (act * up_pre).astype(jnp.bfloat16)
    tangent = (slope * tan_gate * up_pre + act * tan_up).astype(jnp.bfloat16)
    jvp = contract_first(down_rows, tangent) + contract_first(probe_down, hidden) * inv_ff
    positions = jnp.arange(TOKENS, dtype=jnp.int32)
    seq_ids = positions // LEN
    live = (positions % LEN < lengths[seq_ids]).astype(jnp.float32)
    loss_t = (jvp * live[None, :]).astype(jnp.bfloat16)
    back = jnp.dot(down_rows, loss_t, preferred_element_type=jnp.float32)
    s_term = (back * up_pre * slope).astype(jnp.bfloat16)
    r_term = (back * act).astype(jnp.bfloat16)
    grad_gate = jnp.dot(s_term, normed, preferred_element_type=jnp.float32) * inv_d
    grad_up = jnp.dot(r_term, normed, preferred_element_type=jnp.float32) * inv_d
    grad_down = contract_last(hidden, loss_t) * inv_ff
    count = 3.0 * D * FF

    def project(parts):
        total = jnp.sum(parts[0].astype(jnp.float32) * grad_gate)
        total = total + jnp.sum(parts[1].astype(jnp.float32) * grad_up)
        total = total + jnp.sum(parts[2].astype(jnp.float32) * grad_down)
        return total
    proj = lax.map(project, (krylov_gate, krylov_up, krylov_down)) / count

    def remove(carry, items):
        weight, kg, ku, kd = items
        return ((carry[0] - weight * kg.astype(jnp.float32), carry[1] - weight * ku.astype(jnp.float32), carry[2] - weight * kd.astype(jnp.float32)), None)
    (res_gate, res_up, res_down), unused = lax.scan(remove, (grad_gate, grad_up, grad_down), (proj, krylov_gate, krylov_up, krylov_down))
    squares = (jnp.sum(res_gate * res_gate) + jnp.sum(res_up * res_up) + jnp.sum(res_down * res_down)) / count
    norm = jnp.sqrt(squares + 1e-06)
    new_gate = (res_gate / norm).astype(jnp.bfloat16)
    new_up = (res_up / norm).astype(jnp.bfloat16)
    new_down = (res_down / norm).astype(jnp.bfloat16)
    coefficients = jnp.concatenate([proj, norm[None]])
    return (new_gate, new_up, new_down, coefficients)
```

```python
import functools
import math

import jax
import jax.numpy as jnp
from jax import lax
from jax.experimental import pallas as pl
from jax.experimental.pallas import tpu as pltpu
from jax.sharding import PartitionSpec as P

MESH = pl.DeviceIdType.MESH
F32 = jnp.float32
BF16 = jnp.bfloat16
GRAM = 16


def sides(devices):
    return {256: (8, 4), 16: (2, 2)}[devices]


def gelu_pair(gate_pre):
    coef = math.sqrt(2.0 / math.pi)
    cube = gate_pre * gate_pre * gate_pre
    tanh_val = jnp.tanh(coef * (gate_pre + 0.044715 * cube))
    act = 0.5 * gate_pre * (1.0 + tanh_val)
    slope = 0.5 * (1.0 + tanh_val) + 0.5 * gate_pre * (1.0 - tanh_val * tanh_val) * coef * (
        1.0 + 3.0 * 0.044715 * gate_pre * gate_pre
    )
    return (act, slope)


def mm(left, right):
    return jnp.dot(left, right, preferred_element_type=F32)


def mm_last(left, right):
    return lax.dot_general(left, right, (((1,), (1,)), ((), ())), preferred_element_type=F32)


def fold(value):
    rows = value.shape[0]
    total = value[0:8]
    for start in range(8, rows, 8):
        total = total + value[start : start + 8]
    return total


def body(
    cfg,
    len_ref,
    x_hbm,
    gain_hbm,
    gate_hbm,
    up_hbm,
    down_hbm,
    kg_hbm,
    ku_hbm,
    kd_hbm,
    og_hbm,
    ou_hbm,
    od_hbm,
    coef_ref,
    x_v,
    gain_v,
    gate_v,
    up_v,
    down_v,
    k_v,
    rowbuf,
    rows32,
    tok,
    w4,
    sel,
    nc,
    pre,
    psend,
    precv,
    own,
    asend,
    arecv,
    bsend,
    brecv,
    zsum,
    zrecv,
    lz,
    loss,
    backacc,
    w_v,
    gacc,
    qrows,
    sc_p,
    sc_x,
    sc_y,
    sc_z,
    sc_v,
    out_v,
    lsem,
    ksem,
    osem,
    s1,
    r1,
    s2,
    r2,
    s3,
    r3,
):
    Z, A, D, T, L, F, BASIS = cfg
    H = D // 2
    W = H // A
    RZ = L // Z
    R = D // 128
    CH = min(512, D)
    LEN = T // 2
    inv_d = 1.0 / math.sqrt(D)
    inv_ff = 1.0 / math.sqrt(F * T)
    inv_count = 1.0 / (3.0 * D * F * T)
    plane = 2 * A * A

    me = lax.axis_index("fsdp")
    c = lax.rem(me, 2)
    y = lax.rem(me // 2, A)
    x = lax.rem(me // (2 * A), A)
    z = me // plane
    sa = 2 * A - (2 * A - 2) * c
    sb = 2 + (2 * A - 2) * c
    a = x + c * (y - x)
    b = y + c * (x - y)
    partner = me + 1 - 2 * c

    def step(i, k, n):
        return lax.rem(i + k, n)

    def back_of(i, k, n):
        return lax.rem(i + n - k, n)

    def dev_z(k):
        return me + (step(z, k, Z) - z) * plane

    def dev_a(k):
        return me + (step(a, k, A) - a) * sa

    def dev_b(k):
        return me + (step(b, k, A) - b) * sb

    def dev_x(k):
        return me + (step(x, k, A) - x) * (2 * A)

    def dev_y(k):
        return me + (step(y, k, A) - y) * 2

    pending = []

    def send(src, dst, ss, rs, dev):
        cp = pltpu.make_async_remote_copy(
            src_ref=src, dst_ref=dst, send_sem=ss, recv_sem=rs, device_id=(dev,), device_id_type=MESH
        )
        cp.start()
        pending.append(cp)
        return cp

    loads = []
    for i, (src, dst) in enumerate(
        ((x_hbm, x_v), (gain_hbm, gain_v), (gate_hbm, gate_v), (up_hbm, up_v), (down_hbm, down_v))
    ):
        cp = pltpu.make_async_copy(src, dst, lsem.at[i])
        cp.start()
        loads.append(cp)
    kloads = []
    for i, src in enumerate((kg_hbm, ku_hbm, kd_hbm)):
        cp = pltpu.make_async_copy(src, k_v.at[i], ksem.at[i])
        cp.start()
        kloads.append(cp)

    barrier = pltpu.get_barrier_semaphore()
    peers = [dev_z(k) for k in range(1, Z)]
    peers += [dev_a(k) for k in range(1, A)] + [dev_b(k) for k in range(1, A)] + [partner]
    for peer in peers:
        pl.semaphore_signal(barrier, inc=1, device_id=(peer,), device_id_type=MESH)

    loads[0].wait()
    loads[1].wait()
    wide = x_v[...].astype(F32)
    square = jnp.sum(jnp.sum(wide * wide, axis=1, keepdims=True), axis=0, keepdims=True)
    normed_own = wide * lax.rsqrt(square * (1.0 / D) + 1e-06) * gain_v[...].astype(F32)
    rowbuf[z, a] = normed_own.astype(BF16)

    gacc[...] = jnp.zeros_like(gacc)

    def gram(part):
        def chunk(i, carry):
            cols = pl.ds(pl.multiple_of(i * 128, 128), 128)
            ks = [k_v[part, j, :, cols].astype(F32) for j in range(BASIS)]
            n = 0
            for i1 in range(BASIS):
                for j1 in range(i1, BASIS):
                    gacc[n] += fold(ks[i1] * ks[j1])
                    n += 1
            return carry

        lax.fori_loop(0, D // 128, chunk, 0)

    pl.semaphore_wait(barrier, len(peers))

    cps = []
    for k in range(1, Z):
        cps.append(send(rowbuf.at[z, a], rowbuf.at[z, a], s1.at[k - 1], r1.at[k - 1], dev_z(k)))
    kloads[0].wait()
    gram(0)
    for cp in cps:
        cp.wait_recv()
    cps = []
    o = Z - 1
    for k in range(1, A):
        cps.append(
            send(rowbuf.at[:, a], rowbuf.at[:, a], s1.at[o + k - 1], r1.at[o + k - 1], dev_a(k))
        )
    kloads[1].wait()
    gram(1)
    for cp in cps:
        cp.wait_recv()
    for i in range(Z):
        for j in range(A):
            rows32[pl.ds((i * A + j) * R, R), :] = rowbuf[i, j].astype(F32)
    for d in range(R):
        tok[c, b, :, pl.ds(d * 128, 128)] = rows32[pl.ds(d, Z * A, stride=R), :].astype(BF16)
    cps = []
    o += A - 1
    for k in range(1, A):
        cps.append(send(tok.at[c, b], tok.at[c, b], s1.at[o + k - 1], r1.at[o + k - 1], dev_b(k)))
    o += A - 1
    pairs = [send(tok.at[c, b], tok.at[c, b], s1.at[o], r1.at[o], partner)]
    kloads[2].wait()
    gram(2)
    loads[2].wait()
    loads[3].wait()
    loads[4].wait()

    def stack(i, carry):
        cols = pl.ds(pl.multiple_of(i * CH, CH), CH)
        parts = [gate_v[:, cols], up_v[:, cols], k_v[0, BASIS - 1, :, cols], k_v[1, BASIS - 1, :, cols]]
        w4[:, cols] = jnp.concatenate([p.astype(F32) for p in parts], axis=0).astype(BF16)
        return carry

    lax.fori_loop(0, D // CH, stack, 0)
    len0 = len_ref[0]
    len1 = len_ref[1]
    col = lax.broadcasted_iota(jnp.int32, (L, T), 1)
    row = lax.broadcasted_iota(jnp.int32, (L, T), 0)
    gc = col // (T // 2)
    gb = lax.rem(col // (Z * A), A)
    gz = lax.rem(col // A, Z)
    ga = lax.rem(col, A)
    gx = ga + gc * (gb - ga)
    gy = gb + gc * (ga - gb)
    token = gz * plane + gx * (2 * A) + gy * 2 + gc
    second = token >= LEN
    inner = jnp.where(second, token - LEN, token)
    live = inner < jnp.where(second, len1, len0)
    place = jnp.where(live, inner + jnp.where(second, len0, 0), -1)
    hit = place == row
    sel[...] = jnp.where(hit, 1.0, 0.0).astype(BF16)
    for k in range(1, A):
        cps[k - 1].wait_recv()
        kb = back_of(b, k, A)
        pairs.append(send(tok.at[c, kb], tok.at[c, kb], s1.at[o + k], r1.at[o + k], partner))
    for cp in pairs:
        cp.wait_recv()

    pre[...] = jnp.zeros_like(pre)

    def first(i, carry):
        cols = pl.ds(pl.multiple_of(i * CH, CH), CH)
        every = tok[:, :, :, cols].reshape(T, CH)
        kept = mm(sel[...], every).astype(BF16)
        nc[:, cols] = kept
        pre[...] += mm_last(w4[:, cols], kept)
        return carry

    lax.fori_loop(0, D // CH, first, 0)
    gate_pre = pre[0:F]
    up_pre = pre[F : 2 * F]
    tan_gate = pre[2 * F : 3 * F] * inv_d
    tan_up = pre[3 * F : 4 * F] * inv_d
    act, slope = gelu_pair(gate_pre)
    hidden = act * up_pre
    tangent = slope * tan_gate * up_pre + act * tan_up
    hid_t = hidden.T.astype(BF16)
    tan_t = tangent.T.astype(BF16)

    def jvp_block(start):
        cols = pl.ds(pl.multiple_of(start, 128), W)
        return mm(tan_t, down_v[:, cols]) + mm(hid_t, k_v[2, BASIS - 1, :, cols]) * inv_ff

    order = list(range(1, A)) + [0]
    pcps = [None] * A
    for k in order:
        psend[k] = jvp_block((1 - c) * H + step(b, k, A) * W).astype(BF16)
        pcps[k] = send(psend.at[k], precv.at[k], s2.at[k], r2.at[k], partner)
    o = A
    for k in order:
        own[k] = jvp_block(c * H + step(a, k, A) * W)
    acps = []
    for k in order:
        pcps[k].wait_recv()
        total = own[k] + precv[k].astype(F32)
        if k:
            asend[k - 1] = total.astype(BF16)
            acps.append(send(asend.at[k - 1], arecv.at[k - 1], s2.at[o + k - 1], r2.at[o + k - 1], dev_a(k)))
        else:
            own[0] = total
    o += A - 1
    for cp in acps:
        cp.wait_recv()
    bcps = []
    for k in order:
        cols = pl.ds(pl.multiple_of(step(b, k, A) * 128, 128), 128)
        total = own[0, :, cols]
        for j in range(A - 1):
            total = total + arecv[j, :, cols].astype(F32)
        if k:
            bsend[k - 1] = total.astype(BF16)
            bcps.append(send(bsend.at[k - 1], brecv.at[k - 1], s2.at[o + k - 1], r2.at[o + k - 1], dev_b(k)))
        else:
            kept = total
    o += A - 1
    for cp in bcps:
        cp.wait_recv()
    for j in range(A - 1):
        kept = kept + brecv[j].astype(F32)
    zsum[...] = kept
    zcps = []
    for k in range(1, Z):
        rows = pl.ds(pl.multiple_of(step(z, k, Z) * RZ, RZ), RZ)
        zcps.append(send(zsum.at[rows], zrecv.at[k - 1], s2.at[o + k - 1], r2.at[o + k - 1], dev_z(k)))
    o += Z - 1
    mine = pl.ds(pl.multiple_of(z * RZ, RZ), RZ)
    for cp in zcps:
        cp.wait_recv()
    total = zsum[mine, :]
    for j in range(Z - 1):
        total = total + zrecv[j]
    lz[mine, :] = total.astype(BF16).astype(F32)

    zcps = []
    for k in range(1, Z):
        zcps.append(send(lz.at[mine], lz.at[mine], s3.at[k - 1], r3.at[k - 1], dev_z(k)))
    o = Z - 1
    for cp in zcps:
        cp.wait_recv()

    def block(ai, bi):
        return pl.ds(pl.multiple_of(c * H + ai * W + bi * 128, 128), 128)

    here = block(a, b)
    loss[:, here] = lz[...].astype(BF16)
    bcps = []
    for k in range(1, A):
        bcps.append(send(loss.at[:, here], loss.at[:, here], s3.at[o + k - 1], r3.at[o + k - 1], dev_b(k)))
    o += A - 1
    oa = o
    op = oa + A * (A - 1)
    acps = {}
    gcps = {}

    def pass_on(kb):
        ref = loss.at[:, block(a, back_of(b, kb, A))]
        for k in range(1, A):
            n = oa + kb * (A - 1) + k - 1
            acps[k, kb] = send(ref, ref, s3.at[n], r3.at[n], dev_a(k))
        gcps[0, kb] = send(ref, ref, s3.at[op + kb], r3.at[op + kb], partner)

    pass_on(0)
    for kb in range(1, A):
        bcps[kb - 1].wait_recv()
        pass_on(kb)
    for kb in range(A):
        for ka in range(1, A):
            acps[ka, kb].wait_recv()
            ref = loss.at[:, block(back_of(a, ka, A), back_of(b, kb, A))]
            n = op + ka * A + kb
            gcps[ka, kb] = send(ref, ref, s3.at[n], r3.at[n], partner)
    o = op + A * A
    for kb in range(A):
        for ka in range(A):
            gcps[ka, kb].wait_recv()

    backacc[...] = jnp.zeros_like(backacc)

    def second_pass(i, carry):
        cols = pl.ds(pl.multiple_of(i * CH, CH), CH)
        backacc[...] += mm_last(down_v[:, cols], loss[:, cols])
        return carry

    lax.fori_loop(0, D // CH, second_pass, 0)
    back = backacc[...]
    gate_pre = pre[0:F]
    up_pre = pre[F : 2 * F]
    act, slope = gelu_pair(gate_pre)
    hid = (act * up_pre).astype(BF16)
    both = jnp.concatenate([back * up_pre * slope, back * act], axis=0).astype(BF16)

    def grads(i, carry):
        cols = pl.ds(pl.multiple_of(i * CH, CH), CH)
        two = mm(both, nc[:, cols]) * inv_d
        three = mm(hid, loss[:, cols]) * inv_ff
        parts = (two[0:F], two[F : 2 * F], three)
        carry = list(carry)
        for part in range(3):
            grad = parts[part]
            w_v[part, :, cols] = grad
            for sub in range(CH // 128):
                g = grad[:, sub * 128 : (sub + 1) * 128]
                scols = pl.ds(pl.multiple_of(i * CH + sub * 128, 128), 128)
                for j in range(BASIS):
                    carry[j] = carry[j] + fold(k_v[part, j, :, scols].astype(F32) * g)
                carry[BASIS] = carry[BASIS] + fold(g * g)
        return tuple(carry)

    zero = jnp.zeros((8, 128), F32)
    sums = lax.fori_loop(0, D // CH, grads, (zero,) * (BASIS + 1))
    qrows[...] = jnp.zeros_like(qrows)
    for j in range(BASIS + 1):
        qrows[j : j + 1, :] = jnp.sum(sums[j], axis=0, keepdims=True)
    n = 0
    for i1 in range(BASIS):
        for j1 in range(i1, BASIS):
            q = GRAM + i1 * BASIS + j1
            qrows[q : q + 1, :] = jnp.sum(gacc[n], axis=0, keepdims=True)
            n += 1
    line = jnp.sum(qrows[...], axis=1, keepdims=True) * inv_count
    rowi = lax.broadcasted_iota(jnp.int32, (128, 128), 0)
    coli = lax.broadcasted_iota(jnp.int32, (128, 128), 1)
    tile = jnp.sum(jnp.where(rowi == coli, line, 0.0), axis=0, keepdims=True)
    tile = jnp.broadcast_to(tile, (8, 128))

    def share(slots, value, at, size, o, dev):
        slots[at] = value
        cps = []
        for k in range(1, size):
            cps.append(send(slots.at[at], slots.at[at], s3.at[o + k - 1], r3.at[o + k - 1], dev(k)))
        for cp in cps:
            cp.wait_recv()
        total = slots[0]
        for j in range(1, size):
            total = total + slots[j]
        return total

    tile = share(sc_p, tile, c, 2, o, lambda k: partner)
    o += 1
    tile = share(sc_x, tile, x, A, o, dev_x)
    o += A - 1
    tile = share(sc_y, tile, y, A, o, dev_y)
    o += A - 1
    tile = share(sc_z, tile, z, Z, o, dev_z)
    o += Z - 1

    tile = tile[0:1]
    lane = lax.broadcasted_iota(jnp.int32, (1, 128), 1)
    proj = [
        jnp.sum(jnp.where(lane == j, tile, 0.0), axis=1, keepdims=True) for j in range(BASIS)
    ]
    gi = (lane - GRAM) // BASIS
    gj = lax.rem(lane + (8 * BASIS - GRAM), BASIS)
    left = jnp.zeros_like(tile)
    right = jnp.zeros_like(tile)
    for j in range(BASIS):
        left = left + jnp.where(gi == j, proj[j], 0.0)
        right = right + jnp.where(gj == j, proj[j], 0.0)
    inside = (lane >= GRAM) & (lane < GRAM + BASIS * BASIS)
    weight = jnp.where(inside, jnp.where(gi == gj, 1.0, 2.0), 0.0)
    terms = left * right * tile * weight
    terms = terms + jnp.where(lane == BASIS, tile, 0.0)
    terms = terms - jnp.where(lane < BASIS, 2.0 * tile * tile, 0.0)
    squares = jnp.maximum(jnp.sum(terms, axis=1, keepdims=True), 0.0)
    norm = jnp.sqrt(squares + 1e-06)
    inv_norm = 1.0 / norm
    coef_ref[...] = jnp.where(lane == BASIS, norm, tile)

    outs = []
    for part, dst in enumerate((og_hbm, ou_hbm, od_hbm)):

        def final(i, carry, part=part):
            cols = pl.ds(pl.multiple_of(i * 256, 256), 256)
            left_over = w_v[part, :, cols]
            for j in range(BASIS):
                left_over = left_over - proj[j] * k_v[part, j, :, cols].astype(F32)
            out_v[part, :, cols] = (left_over * inv_norm).astype(BF16)
            return carry

        lax.fori_loop(0, D // 256, final, 0)
        cp = pltpu.make_async_copy(out_v.at[part], dst, osem.at[part])
        cp.start()
        outs.append(cp)
    for cp in pending:
        cp.wait_send()
    for cp in outs:
        cp.wait()


def per_device(
    inputs, norm_gain, lengths, gate_rows, up_rows, down_rows, krylov_gate, krylov_up, krylov_down
):
    devices = lax.axis_size("fsdp")
    Z, A = sides(devices)
    D = inputs.shape[1]
    T = inputs.shape[0] * devices
    L = T * 3 // 4
    BASIS, F, _ = krylov_gate.shape
    R = D // 128
    H = D // 2
    W = H // A
    cfg = (Z, A, D, T, L, F, BASIS)
    pairs = BASIS * (BASIS + 1) // 2
    n1 = Z - 1 + 2 * (A - 1) + A
    n2 = A + 2 * (A - 1) + Z - 1
    n3 = Z - 1 + A - 1 + A * (A - 1) + A * A + 1 + 2 * (A - 1) + Z - 1
    hbm = pl.BlockSpec(memory_space=pl.ANY)
    part = jax.ShapeDtypeStruct((F, D), BF16)
    dma = pltpu.SemaphoreType.DMA
    out = pl.pallas_call(
        functools.partial(body, cfg),
        out_shape=(part, part, part, jax.ShapeDtypeStruct((1, 128), F32)),
        in_specs=[pl.BlockSpec(memory_space=pltpu.SMEM)] + [hbm] * 8,
        out_specs=(hbm, hbm, hbm, pl.BlockSpec(memory_space=pltpu.VMEM)),
        scratch_shapes=[
            pltpu.VMEM((R, 128), BF16),
            pltpu.VMEM((R, 128), BF16),
            pltpu.VMEM((F, D), BF16),
            pltpu.VMEM((F, D), BF16),
            pltpu.VMEM((F, D), BF16),
            pltpu.VMEM((3, BASIS, F, D), BF16),
            pltpu.VMEM((Z, A, R, 128), BF16),
            pltpu.VMEM((Z * A * R, 128), F32),
            pltpu.VMEM((2, A, Z * A, D), BF16),
            pltpu.VMEM((4 * F, D), BF16),
            pltpu.VMEM((L, T), BF16),
            pltpu.VMEM((L, D), BF16),
            pltpu.VMEM((4 * F, L), F32),
            pltpu.VMEM((A, L, W), BF16),
            pltpu.VMEM((A, L, W), BF16),
            pltpu.VMEM((A, L, W), F32),
            pltpu.VMEM((A - 1, L, W), BF16),
            pltpu.VMEM((A - 1, L, W), BF16),
            pltpu.VMEM((A - 1, L, 128), BF16),
            pltpu.VMEM((A - 1, L, 128), BF16),
            pltpu.VMEM((L, 128), F32),
            pltpu.VMEM((Z - 1, L // Z, 128), F32),
            pltpu.VMEM((L, 128), F32),
            pltpu.VMEM((L, D), BF16),
            pltpu.VMEM((F, L), F32),
            pltpu.VMEM((3, F, D), F32),
            pltpu.VMEM((pairs, 8, 128), F32),
            pltpu.VMEM((128, 128), F32),
            pltpu.VMEM((2, 8, 128), F32),
            pltpu.VMEM((A, 8, 128), F32),
            pltpu.VMEM((A, 8, 128), F32),
            pltpu.VMEM((Z, 8, 128), F32),
            pltpu.VMEM((8, 128), F32),
            pltpu.VMEM((3, F, D), BF16),
            dma((5,)),
            dma((3,)),
            dma((3,)),
            dma((n1,)),
            dma((n1,)),
            dma((n2,)),
            dma((n2,)),
            dma((n3,)),
            dma((n3,)),
        ],
        compiler_params=pltpu.CompilerParams(
            collective_id=0, has_side_effects=True, vmem_limit_bytes=60 << 20
        ),
        name="arnoldi_step",
    )(
        lengths,
        inputs.reshape(R, 128),
        norm_gain.reshape(R, 128),
        gate_rows,
        up_rows,
        down_rows,
        krylov_gate,
        krylov_up,
        krylov_down,
    )
    return (out[0], out[1], out[2], out[3][0, : BASIS + 1])


def solution(mesh):
    placed = (
        P("fsdp", None),
        P(),
        P(),
        P("fsdp", None),
        P("fsdp", None),
        P("fsdp", None),
        P(None, "fsdp", None),
        P(None, "fsdp", None),
        P(None, "fsdp", None),
    )
    return jax.shard_map(
        per_device,
        mesh=mesh,
        in_specs=placed,
        out_specs=(P("fsdp", None), P("fsdp", None), P("fsdp", None), P()),
        check_vma=False,
    )
```

```python
import functools
import math

import jax
import jax.numpy as jnp
from jax import lax
from jax.experimental import pallas as pl
from jax.experimental.pallas import tpu as pltpu
from jax.sharding import PartitionSpec as P

MESH = pl.DeviceIdType.MESH
F32 = jnp.float32
BF16 = jnp.bfloat16
GRAM = 16


def sides(devices):
    return {256: (8, 4), 16: (2, 2)}[devices]


def gelu_pair(gate_pre):
    coef = math.sqrt(2.0 / math.pi)
    cube = gate_pre * gate_pre * gate_pre
    tanh_val = jnp.tanh(coef * (gate_pre + 0.044715 * cube))
    act = 0.5 * gate_pre * (1.0 + tanh_val)
    slope = 0.5 * (1.0 + tanh_val) + 0.5 * gate_pre * (1.0 - tanh_val * tanh_val) * coef * (
        1.0 + 3.0 * 0.044715 * gate_pre * gate_pre
    )
    return (act, slope)


def mm(left, right):
    return jnp.dot(left, right, preferred_element_type=F32)


def mm_last(left, right):
    return lax.dot_general(left, right, (((1,), (1,)), ((), ())), preferred_element_type=F32)


def fold(value):
    rows = value.shape[0]
    total = value[0:8]
    for start in range(8, rows, 8):
        total = total + value[start : start + 8]
    return total


def near_first(count):
    return {8: (0, 1, 7, 2, 6, 3, 5, 4), 2: (0, 1)}[count]


def body(
    cfg,
    len_ref,
    x_hbm,
    gain_hbm,
    gate_hbm,
    up_hbm,
    down_hbm,
    kg_hbm,
    ku_hbm,
    kd_hbm,
    w_v,
    k_v,
    coef_ref,
    x_v,
    gain_v,
    gate_v,
    up_v,
    down_v,
    x32,
    rowbuf,
    rows32,
    tok,
    w4,
    sel,
    nc,
    every,
    pre,
    psend,
    precv,
    own,
    asend,
    arecv,
    bsend,
    brecv,
    zsum,
    zrecv,
    lz,
    loss,
    backacc,
    gacc,
    qrows,
    sc_zc,
    sc_xy,
    lsem,
    ksem,
    s1,
    r1,
    s2,
    r2,
    s3,
    r3,
    s4,
    r4,
):
    Z, A, D, T, L, F, BASIS = cfg
    H = D // 2
    W = H // A
    RZ = L // Z
    R = D // 128
    CH = min(512, D)
    LEN = T // 2
    HZ = Z // 2
    HL = L // 2
    NEAR = near_first(Z)
    SLOT = {k: g for g, k in enumerate(NEAR)}
    inv_d = 1.0 / math.sqrt(D)
    inv_ff = 1.0 / math.sqrt(F * T)
    inv_count = 1.0 / (3.0 * D * F * T)
    plane = 2 * A * A

    me = lax.axis_index("fsdp")
    c = lax.rem(me, 2)
    y = lax.rem(me // 2, A)
    x = lax.rem(me // (2 * A), A)
    z = me // plane
    sa = 2 * A - (2 * A - 2) * c
    sb = 2 + (2 * A - 2) * c
    a = x + c * (y - x)
    b = y + c * (x - y)
    partner = me + 1 - 2 * c

    def step(i, k, n):
        return lax.rem(i + k, n)

    def back_of(i, k, n):
        return lax.rem(i + n - k, n)

    def dev_z(k):
        return me + (step(z, k, Z) - z) * plane

    def dev_a(k):
        return me + (step(a, k, A) - a) * sa

    def dev_b(k):
        return me + (step(b, k, A) - b) * sb

    def dev_zc(k, flip):
        return dev_z(k) + flip * (1 - 2 * c)

    def dev_xy(kx, ky):
        return me + (step(x, kx, A) - x) * (2 * A) + (step(y, ky, A) - y) * 2

    pending = []

    def send(src, dst, ss, rs, dev):
        cp = pltpu.make_async_remote_copy(
            src_ref=src, dst_ref=dst, send_sem=ss, recv_sem=rs, device_id=(dev,), device_id_type=MESH
        )
        cp.start()
        pending.append(cp)
        return cp

    zc_group = [(k, flip) for k in range(Z) for flip in range(2) if k or flip]
    xy_group = [(kx, ky) for kx in range(A) for ky in range(A) if kx or ky]
    barrier = pltpu.get_barrier_semaphore()
    peers = [dev_zc(k, flip) for k, flip in zc_group] + [dev_xy(kx, ky) for kx, ky in xy_group]
    for peer in peers:
        pl.semaphore_signal(barrier, inc=1, device_id=(peer,), device_id_type=MESH)

    loads = []
    for i, (src, dst) in enumerate(
        ((x_hbm, x_v), (gain_hbm, gain_v), (gate_hbm, gate_v), (up_hbm, up_v), (down_hbm, down_v))
    ):
        cp = pltpu.make_async_copy(src, dst, lsem.at[i])
        cp.start()
        loads.append(cp)
    kloads = []
    for i, src in enumerate((kg_hbm, ku_hbm, kd_hbm)):
        cp = pltpu.make_async_copy(src, k_v.at[i], ksem.at[i])
        cp.start()
        kloads.append(cp)

    loads[0].wait()
    loads[1].wait()
    flat = x_v[...].astype(F32)
    for d in range(R):
        x32[d : d + 1, :] = flat[:, d * 128 : (d + 1) * 128]
    wide = x32[...]
    square = jnp.sum(jnp.sum(wide * wide, axis=1, keepdims=True), axis=0, keepdims=True)
    normed_own = wide * lax.rsqrt(square * (1.0 / D) + 1e-06) * gain_v[...].astype(F32)
    rowbuf[0, a] = normed_own.astype(BF16)

    gacc[...] = jnp.zeros_like(gacc)

    def gram(part):
        def chunk(i, carry):
            cols = pl.ds(pl.multiple_of(i * 128, 128), 128)
            ks = [k_v[part, j, :, cols].astype(F32) for j in range(BASIS)]
            n = 0
            for i1 in range(BASIS):
                for j1 in range(i1, BASIS):
                    gacc[n] += fold(ks[i1] * ks[j1])
                    n += 1
            return carry

        lax.fori_loop(0, D // 128, chunk, 0)

    pl.semaphore_wait(barrier, len(peers))

    zcps = {}
    for k in NEAR[1:]:
        g = SLOT[Z - k]
        zcps[g] = send(rowbuf.at[0, a], rowbuf.at[g, a], s1.at[g], r1.at[g], dev_z(k))
    o = Z

    def sem1(group, n):
        return o + group * n

    base = Z
    acps = [None, None]
    for h in range(2):
        for g in range(max(1, h * HZ), (h + 1) * HZ):
            zcps[g].wait_recv()
        mine = rowbuf.at[pl.ds(h * HZ, HZ), a]
        acps[h] = []
        for k in range(1, A):
            n = base + h * (A - 1) + k - 1
            acps[h].append(send(mine, mine, s1.at[n], r1.at[n], dev_a(k)))
        if h == 0:
            kloads[0].wait()
    base += 2 * (A - 1)
    bcps = [None, None]
    pcps = [[], []]
    pbase = base + 2 * (A - 1)
    for h in range(2):
        for cp in acps[h]:
            cp.wait_recv()
        for i in range(HZ):
            for j in range(A):
                rows32[pl.ds((i * A + j) * R, R), :] = rowbuf[h * HZ + i, j].astype(F32)
        for d in range(R):
            tok[h, c, b, :, pl.ds(d * 128, 128)] = rows32[pl.ds(d, HZ * A, stride=R), :].astype(BF16)
        mine = tok.at[h, c, b]
        bcps[h] = []
        for k in range(1, A):
            n = base + h * (A - 1) + k - 1
            bcps[h].append(send(mine, mine, s1.at[n], r1.at[n], dev_b(k)))
        n = pbase + h * A
        pcps[h].append(send(mine, mine, s1.at[n], r1.at[n], partner))
    gram(0)
    kloads[1].wait()
    loads[2].wait()
    loads[3].wait()
    loads[4].wait()

    def stack(i, carry):
        cols = pl.ds(pl.multiple_of(i * CH, CH), CH)
        parts = [gate_v[:, cols], up_v[:, cols], k_v[0, BASIS - 1, :, cols], k_v[1, BASIS - 1, :, cols]]
        w4[:, cols] = jnp.concatenate([p.astype(F32) for p in parts], axis=0).astype(BF16)
        return carry

    lax.fori_loop(0, D // CH, stack, 0)
    len0 = len_ref[0]
    len1 = len_ref[1]
    col = lax.broadcasted_iota(jnp.int32, (L, T), 1)
    row = lax.broadcasted_iota(jnp.int32, (L, T), 0)

    def offset(g):
        k = jnp.zeros_like(g)
        for slot in range(1, Z):
            k = jnp.where(g == slot, NEAR[slot], k)
        return lax.rem(k + z, Z)

    gh = col // (T // 2)
    gc = lax.rem(col // (T // 4), 2)
    gb = lax.rem(col // (HZ * A), A)
    gz = offset(gh * HZ + lax.rem(col // A, HZ))
    ga = lax.rem(col, A)
    gx = ga + gc * (gb - ga)
    gy = gb + gc * (ga - gb)
    token = gz * plane + gx * (2 * A) + gy * 2 + gc
    second = token >= LEN
    inner = jnp.where(second, token - LEN, token)
    live = inner < jnp.where(second, len1, len0)
    place = jnp.where(live, inner + jnp.where(second, len0, 0), -1)
    wanted = offset(row // RZ) * RZ + lax.rem(row, RZ)
    sel[...] = jnp.where(place == wanted, 1.0, 0.0).astype(BF16)
    for h in range(2):
        for k in range(1, A):
            bcps[h][k - 1].wait_recv()
            ref = tok.at[h, c, back_of(b, k, A)]
            n = pbase + h * A + k
            pcps[h].append(send(ref, ref, s1.at[n], r1.at[n], partner))
        if h == 0:
            gram(1)

    every[...] = jnp.zeros_like(every)
    for h in range(2):
        for cp in pcps[h]:
            cp.wait_recv()

        def first(i, carry, h=h):
            cols = pl.ds(pl.multiple_of(i * CH, CH), CH)
            half = tok[h, :, :, :, cols].reshape(T // 2, CH)
            every[h] += mm_last(w4[:, cols], half)
            return carry

        lax.fori_loop(0, D // CH, first, 0)
    whole = jnp.concatenate([every[0], every[1]], axis=1)
    moved = None
    for _ in range(3):
        term = whole.astype(BF16)
        whole = whole - term.astype(F32)
        term = mm_last(term, sel[...])
        moved = term if moved is None else moved + term
    pre[...] = moved
    gate_pre = pre[0:F]
    up_pre = pre[F : 2 * F]
    tan_gate = pre[2 * F : 3 * F] * inv_d
    tan_up = pre[3 * F : 4 * F] * inv_d
    act, slope = gelu_pair(gate_pre)
    hidden = act * up_pre
    tangent = slope * tan_gate * up_pre + act * tan_up
    hid_t = hidden.T.astype(BF16)
    tan_t = tangent.T.astype(BF16)
    kloads[2].wait()

    def jvp_block(start):
        cols = pl.ds(pl.multiple_of(start, 128), W)
        return mm(tan_t, down_v[:, cols]) + mm(hid_t, k_v[2, BASIS - 1, :, cols]) * inv_ff

    order = list(range(1, A)) + [0]
    pcps = [None] * A
    for k in order:
        psend[k] = jvp_block((1 - c) * H + step(b, k, A) * W).astype(BF16)
        pcps[k] = send(psend.at[k], precv.at[k], s2.at[k], r2.at[k], partner)
    base = A
    halves = (1, 0)
    acps = [[], []]

    def pass_a(h, k, total):
        if k:
            n = base + h * (A - 1) + k - 1
            asend[h, k - 1] = total.astype(BF16)
            acps[h].append(send(asend.at[h, k - 1], arecv.at[h, k - 1], s2.at[n], r2.at[n], dev_a(k)))
        else:
            own[0, h * HL : (h + 1) * HL, :] = total

    for k in order:
        mine = jvp_block(c * H + step(a, k, A) * W)
        pcps[k].wait_recv()
        total = mine + precv[k].astype(F32)
        own[k] = total
        pass_a(1, k, total[HL:L])
    for k in order:
        pass_a(0, k, own[k, 0:HL, :])
    gram(2)
    base += 2 * (A - 1)
    bcps = [[], []]
    for h in halves:
        rows = slice(h * HL, (h + 1) * HL)
        for cp in acps[h]:
            cp.wait_recv()
        for k in order:
            cols = pl.ds(pl.multiple_of(step(b, k, A) * 128, 128), 128)
            total = own[0, rows, cols]
            for j in range(A - 1):
                total = total + arecv[h, j, :, cols].astype(F32)
            if k:
                n = base + h * (A - 1) + k - 1
                bsend[h, k - 1] = total.astype(BF16)
                bcps[h].append(send(bsend.at[h, k - 1], brecv.at[h, k - 1], s2.at[n], r2.at[n], dev_b(k)))
            else:
                zsum[rows, :] = total
    base += 2 * (A - 1)
    zcps = []
    for h in halves:
        rows = slice(h * HL, (h + 1) * HL)
        for cp in bcps[h]:
            cp.wait_recv()
        total = zsum[rows, :]
        for j in range(A - 1):
            total = total + brecv[h, j].astype(F32)
        zsum[rows, :] = total
        for g in range(max(1, h * HZ), (h + 1) * HZ):
            k = NEAR[g]
            zcps.append(
                send(zsum.at[pl.ds(g * RZ, RZ)], zrecv.at[k - 1], s2.at[base + k], r2.at[base + k], dev_z(k))
            )
    def keep(i, carry):
        cols = pl.ds(pl.multiple_of(i * CH, CH), CH)
        nc[:, cols] = mm(sel[...], tok[:, :, :, :, cols].reshape(T, CH)).astype(BF16)
        return carry

    lax.fori_loop(0, D // CH, keep, 0)
    for cp in zcps:
        cp.wait_recv()
    total = zsum[0:RZ, :]
    for j in range(Z - 1):
        total = total + zrecv[j]
    lz[0] = total.astype(BF16)

    zcps = {}
    for k in NEAR[1:]:
        g = SLOT[Z - k]
        zcps[g] = send(lz.at[0], lz.at[g], s3.at[g], r3.at[g], dev_z(k))
    base = Z
    abase = base + 2 * (A - 1)
    pbase = abase + 2 * A * (A - 1)
    bcps = [[], []]
    acps = {}
    pcps = []

    def pass_on(h, kb):
        ref = loss.at[h, c, a, back_of(b, kb, A)]
        for k in range(1, A):
            n = abase + (h * A + kb) * (A - 1) + k - 1
            acps[h, kb, k] = send(ref, ref, s3.at[n], r3.at[n], dev_a(k))
        n = pbase + h * (2 * A - 1) + kb
        pcps.append(send(ref, ref, s3.at[n], r3.at[n], partner))

    for h in range(2):
        for g in range(max(1, h * HZ), (h + 1) * HZ):
            zcps[g].wait_recv()
        groups = [lz[g].astype(F32) for g in range(h * HZ, (h + 1) * HZ)]
        mine = groups[0] if len(groups) == 1 else jnp.concatenate(groups, axis=0)
        loss[h, c, a, b] = mine.astype(BF16)
        ref = loss.at[h, c, a, b]
        for k in range(1, A):
            n = base + h * (A - 1) + k - 1
            bcps[h].append(send(ref, ref, s3.at[n], r3.at[n], dev_b(k)))
        pass_on(h, 0)
    for h in range(2):
        for kb in range(1, A):
            bcps[h][kb - 1].wait_recv()
            pass_on(h, kb)
    for h in range(2):
        for k in range(1, A):
            for kb in range(A):
                acps[h, kb, k].wait_recv()
            ref = loss.at[h, c, back_of(a, k, A)]
            n = pbase + h * (2 * A - 1) + A + k - 1
            pcps.append(send(ref, ref, s3.at[n], r3.at[n], partner))
    backacc[...] = jnp.zeros_like(backacc)
    PER = CH // 128

    def loss_cols(i):
        halves = []
        for h in range(2):
            blocks = []
            for j in range(PER):
                n = i * PER + j
                blocks.append(loss[h, n // (A * A), lax.rem(n // A, A), lax.rem(n, A)])
            halves.append(jnp.concatenate(blocks, axis=1))
        return jnp.concatenate(halves, axis=0)

    def second_pass(i, carry):
        cols = pl.ds(pl.multiple_of(i * CH, CH), CH)
        backacc[...] += mm_last(down_v[:, cols], loss_cols(i))
        return carry

    count = D // CH // 2
    lax.fori_loop(c * count, c * count + count, second_pass, 0)
    for cp in pcps:
        cp.wait_recv()
    lax.fori_loop((1 - c) * count, (1 - c) * count + count, second_pass, 0)
    back = backacc[...]
    gate_pre = pre[0:F]
    up_pre = pre[F : 2 * F]
    act, slope = gelu_pair(gate_pre)
    hid = (act * up_pre).astype(BF16)
    both = jnp.concatenate([back * up_pre * slope, back * act], axis=0).astype(BF16)

    def grads(i, carry):
        cols = pl.ds(pl.multiple_of(i * CH, CH), CH)
        two = mm(both, nc[:, cols]) * inv_d
        three = mm(hid, loss_cols(i)) * inv_ff
        parts = (two[0:F], two[F : 2 * F], three)
        carry = list(carry)
        for part in range(3):
            grad = parts[part]
            w_v[part, :, cols] = grad
            for sub in range(CH // 128):
                g = grad[:, sub * 128 : (sub + 1) * 128]
                scols = pl.ds(pl.multiple_of(i * CH + sub * 128, 128), 128)
                for j in range(BASIS):
                    carry[j] = carry[j] + fold(k_v[part, j, :, scols].astype(F32) * g)
                carry[BASIS] = carry[BASIS] + fold(g * g)
        return tuple(carry)

    zero = jnp.zeros((8, 128), F32)
    sums = lax.fori_loop(0, D // CH, grads, (zero,) * (BASIS + 1))
    qrows[...] = jnp.zeros_like(qrows)
    for j in range(BASIS + 1):
        qrows[j : j + 1, :] = jnp.sum(sums[j], axis=0, keepdims=True)
    n = 0
    for i1 in range(BASIS):
        for j1 in range(i1, BASIS):
            q = GRAM + i1 * BASIS + j1
            qrows[q : q + 1, :] = jnp.sum(gacc[n], axis=0, keepdims=True)
            n += 1
    line = jnp.sum(qrows[...], axis=1, keepdims=True) * inv_count
    rowi = lax.broadcasted_iota(jnp.int32, (128, 128), 0)
    coli = lax.broadcasted_iota(jnp.int32, (128, 128), 1)
    tile = jnp.sum(jnp.where(rowi == coli, line, 0.0), axis=0, keepdims=True)

    def share(slots, value, at, devs, base):
        slots[at] = value
        cps = []
        for n, dev in enumerate(devs):
            cps.append(send(slots.at[at], slots.at[at], s4.at[base + n], r4.at[base + n], dev))
        for cp in cps:
            cp.wait_recv()
        total = slots[0]
        for j in range(1, len(devs) + 1):
            total = total + slots[j]
        return total

    tile = share(sc_zc, tile, z * 2 + c, [dev_zc(k, flip) for k, flip in zc_group], 0)
    tile = share(sc_xy, tile, x * A + y, [dev_xy(kx, ky) for kx, ky in xy_group], len(zc_group))
    coef_ref[...] = tile
    for cp in pending:
        cp.wait_send()


def finish(cfg, coef_in, w_v, k_v, og_hbm, ou_hbm, od_hbm, coef_ref, out_v, osem):
    D, F, BASIS = cfg
    tile = coef_in[...]
    lane = lax.broadcasted_iota(jnp.int32, (1, 128), 1)
    proj = [
        jnp.sum(jnp.where(lane == j, tile, 0.0), axis=1, keepdims=True) for j in range(BASIS)
    ]
    gi = (lane - GRAM) // BASIS
    gj = lax.rem(lane + (8 * BASIS - GRAM), BASIS)
    left = jnp.zeros_like(tile)
    right = jnp.zeros_like(tile)
    for j in range(BASIS):
        left = left + jnp.where(gi == j, proj[j], 0.0)
        right = right + jnp.where(gj == j, proj[j], 0.0)
    inside = (lane >= GRAM) & (lane < GRAM + BASIS * BASIS)
    weight = jnp.where(inside, jnp.where(gi == gj, 1.0, 2.0), 0.0)
    terms = left * right * tile * weight
    terms = terms + jnp.where(lane == BASIS, tile, 0.0)
    terms = terms - jnp.where(lane < BASIS, 2.0 * tile * tile, 0.0)
    squares = jnp.maximum(jnp.sum(terms, axis=1, keepdims=True), 0.0)
    norm = jnp.sqrt(squares + 1e-06)
    inv_norm = 1.0 / norm
    for j in range(BASIS):
        coef_ref[j] = jnp.sum(jnp.where(lane == j, tile, 0.0))
    coef_ref[BASIS] = jnp.sum(jnp.where(lane == 0, norm, 0.0))

    outs = []
    for part, dst in enumerate((og_hbm, ou_hbm, od_hbm)):

        def final(i, carry, part=part):
            cols = pl.ds(pl.multiple_of(i * 256, 256), 256)
            left_over = w_v[part, :, cols]
            for j in range(BASIS):
                left_over = left_over - proj[j] * k_v[part, j, :, cols].astype(F32)
            out_v[part, :, cols] = (left_over * inv_norm).astype(BF16)
            return carry

        lax.fori_loop(0, D // 256, final, 0)
        cp = pltpu.make_async_copy(out_v.at[part], dst, osem.at[part])
        cp.start()
        outs.append(cp)
    for cp in outs:
        cp.wait()


def per_device(
    inputs, norm_gain, lengths, gate_rows, up_rows, down_rows, krylov_gate, krylov_up, krylov_down
):
    devices = lax.axis_size("fsdp")
    Z, A = sides(devices)
    D = inputs.shape[1]
    T = inputs.shape[0] * devices
    L = T * 3 // 4
    BASIS, F, _ = krylov_gate.shape
    R = D // 128
    H = D // 2
    W = H // A
    HZ = Z // 2
    HL = L // 2
    cfg = (Z, A, D, T, L, F, BASIS)
    pairs = BASIS * (BASIS + 1) // 2
    n1 = Z + 4 * (A - 1) + 2 * A
    n2 = A + 4 * (A - 1) + Z
    n3 = Z + 2 * (A - 1) + 2 * A * (A - 1) + 2 * (2 * A - 1)
    n4 = 2 * Z - 1 + A * A - 1
    hbm = pl.BlockSpec(memory_space=pltpu.HBM)
    vmem = pl.BlockSpec(memory_space=pltpu.VMEM)
    dma = pltpu.SemaphoreType.DMA
    w, k, sums = pl.pallas_call(
        functools.partial(body, cfg),
        out_shape=(
            pltpu.VMEM((3, F, D), F32),
            pltpu.VMEM((3, BASIS, F, D), BF16),
            pltpu.VMEM((1, 128), F32),
        ),
        in_specs=[pl.BlockSpec(memory_space=pltpu.SMEM)] + [hbm] * 8,
        out_specs=(vmem, vmem, vmem),
        scratch_shapes=[
            pltpu.VMEM((1, D), BF16),
            pltpu.VMEM((R, 128), BF16),
            pltpu.VMEM((F, D), BF16),
            pltpu.VMEM((F, D), BF16),
            pltpu.VMEM((F, D), BF16),
            pltpu.VMEM((R, 128), F32),
            pltpu.VMEM((Z, A, R, 128), BF16),
            pltpu.VMEM((HZ * A * R, 128), F32),
            pltpu.VMEM((2, 2, A, HZ * A, D), BF16),
            pltpu.VMEM((4 * F, D), BF16),
            pltpu.VMEM((L, T), BF16),
            pltpu.VMEM((L, D), BF16),
            pltpu.VMEM((2, 4 * F, T // 2), F32),
            pltpu.VMEM((4 * F, L), F32),
            pltpu.VMEM((A, L, W), BF16),
            pltpu.VMEM((A, L, W), BF16),
            pltpu.VMEM((A, L, W), F32),
            pltpu.VMEM((2, A - 1, HL, W), BF16),
            pltpu.VMEM((2, A - 1, HL, W), BF16),
            pltpu.VMEM((2, A - 1, HL, 128), BF16),
            pltpu.VMEM((2, A - 1, HL, 128), BF16),
            pltpu.VMEM((L, 128), F32),
            pltpu.VMEM((Z - 1, L // Z, 128), F32),
            pltpu.VMEM((Z, L // Z, 128), BF16),
            pltpu.VMEM((2, 2, A, A, HL, 128), BF16),
            pltpu.VMEM((F, L), F32),
            pltpu.VMEM((pairs, 8, 128), F32),
            pltpu.VMEM((128, 128), F32),
            pltpu.VMEM((2 * Z, 1, 128), F32),
            pltpu.VMEM((A * A, 1, 128), F32),
            dma((5,)),
            dma((3,)),
            dma((n1,)),
            dma((n1,)),
            dma((n2,)),
            dma((n2,)),
            dma((n3,)),
            dma((n3,)),
            dma((n4,)),
            dma((n4,)),
        ],
        compiler_params=pltpu.CompilerParams(
            collective_id=0, has_side_effects=True, vmem_limit_bytes=57200000
        ),
        name="arnoldi_step",
    )(
        lengths,
        inputs,
        norm_gain.reshape(R, 128),
        gate_rows,
        up_rows,
        down_rows,
        krylov_gate,
        krylov_up,
        krylov_down,
    )
    part = jax.ShapeDtypeStruct((F, D), BF16)
    return pl.pallas_call(
        functools.partial(finish, (D, F, BASIS)),
        out_shape=(part, part, part, jax.ShapeDtypeStruct((BASIS + 1,), F32)),
        in_specs=[vmem, vmem, vmem],
        out_specs=(hbm, hbm, hbm, pl.BlockSpec(memory_space=pltpu.SMEM)),
        scratch_shapes=[pltpu.VMEM((3, F, D), BF16), dma((3,))],
        compiler_params=pltpu.CompilerParams(vmem_limit_bytes=8 << 20),
        name="arnoldi_finish",
    )(sums, w, k)


def solution(mesh):
    placed = (
        P("fsdp", None),
        P(),
        P(),
        P("fsdp", None),
        P("fsdp", None),
        P("fsdp", None),
        P(None, "fsdp", None),
        P(None, "fsdp", None),
        P(None, "fsdp", None),
    )
    return jax.shard_map(
        per_device,
        mesh=mesh,
        in_specs=placed,
        out_specs=(P("fsdp", None), P("fsdp", None), P("fsdp", None), P()),
        check_vma=False,
    )
```

```python
import functools
import math

import jax
import jax.numpy as jnp
from jax import lax
from jax.experimental import pallas as pl
from jax.experimental.pallas import tpu as pltpu
from jax.sharding import PartitionSpec as P

MESH = pl.DeviceIdType.MESH
F32 = jnp.float32
BF16 = jnp.bfloat16
GRAM = 16


def sides(devices):
    return {256: (8, 4), 16: (2, 2)}[devices]


def gelu_pair(gate_pre):
    coef = math.sqrt(2.0 / math.pi)
    cube = gate_pre * gate_pre * gate_pre
    tanh_val = jnp.tanh(coef * (gate_pre + 0.044715 * cube))
    act = 0.5 * gate_pre * (1.0 + tanh_val)
    slope = 0.5 * (1.0 + tanh_val) + 0.5 * gate_pre * (1.0 - tanh_val * tanh_val) * coef * (
        1.0 + 3.0 * 0.044715 * gate_pre * gate_pre
    )
    return (act, slope)


def mm(left, right):
    return jnp.dot(left, right, preferred_element_type=F32)


def mm_last(left, right):
    return lax.dot_general(left, right, (((1,), (1,)), ((), ())), preferred_element_type=F32)


def fold(value):
    rows = value.shape[0]
    total = value[0:8]
    for start in range(8, rows, 8):
        total = total + value[start : start + 8]
    return total


def near_first(count):
    return {8: (0, 1, 7, 2, 6, 3, 5, 4), 2: (0, 1)}[count]


def body(
    cfg,
    len_ref,
    x_hbm,
    gain_hbm,
    gate_hbm,
    up_hbm,
    down_hbm,
    kg_hbm,
    ku_hbm,
    kd_hbm,
    w_v,
    k_v,
    coef_ref,
    x_v,
    gain_v,
    gate_v,
    up_v,
    down_v,
    x32,
    rowbuf,
    rows32,
    tok,
    w4t,
    downt,
    sel,
    nc,
    every,
    pre,
    psend,
    precv,
    own,
    asend,
    arecv,
    bsend,
    brecv,
    zsum,
    zsend,
    zrecv,
    lz,
    loss,
    backacc,
    gacc,
    qrows,
    drows,
    act_v,
    bend_v,
    hid_v,
    sc_zc,
    sc_xy,
    lsem,
    ksem,
    s1,
    r1,
    s2,
    r2,
    s3,
    r3,
    s4,
    r4,
):
    Z, A, D, T, L, F, BASIS = cfg
    H = D // 2
    W = H // A
    RZ = L // Z
    R = D // 128
    CH = min(512, D)
    CW = min(1024, D // 2)
    LEN = T // 2
    HZ = Z // 2
    HL = L // 2
    NEAR = near_first(Z)
    NS = min(2, Z)
    G = Z // NS
    SLOT = {k: g for g, k in enumerate(NEAR)}
    inv_d = 1.0 / math.sqrt(D)
    inv_ff = 1.0 / math.sqrt(F * T)
    inv_count = 1.0 / (3.0 * D * F * T)
    plane = 2 * A * A

    me = lax.axis_index("fsdp")
    c = lax.rem(me, 2)
    y = lax.rem(me // 2, A)
    x = lax.rem(me // (2 * A), A)
    z = me // plane
    sa = 2 * A - (2 * A - 2) * c
    sb = 2 + (2 * A - 2) * c
    a = x + c * (y - x)
    b = y + c * (x - y)
    partner = me + 1 - 2 * c

    def step(i, k, n):
        return lax.rem(i + k, n)

    def back_of(i, k, n):
        return lax.rem(i + n - k, n)

    def dev_z(k):
        return me + (step(z, k, Z) - z) * plane

    def dev_a(k):
        return me + (step(a, k, A) - a) * sa

    def dev_b(k):
        return me + (step(b, k, A) - b) * sb

    def dev_zc(k, flip):
        return dev_z(k) + flip * (1 - 2 * c)

    def dev_xy(kx, ky):
        return me + (step(x, kx, A) - x) * (2 * A) + (step(y, ky, A) - y) * 2

    pending = []

    def send(src, dst, ss, rs, dev):
        cp = pltpu.make_async_remote_copy(
            src_ref=src, dst_ref=dst, send_sem=ss, recv_sem=rs, device_id=(dev,), device_id_type=MESH
        )
        cp.start()
        pending.append(cp)
        return cp

    zc_group = [(k, flip) for k in range(Z) for flip in range(2) if k or flip]
    xy_group = [(kx, ky) for kx in range(A) for ky in range(A) if kx or ky]
    barrier = pltpu.get_barrier_semaphore()
    peers = [dev_zc(k, flip) for k, flip in zc_group] + [dev_xy(kx, ky) for kx, ky in xy_group]
    for peer in peers:
        pl.semaphore_signal(barrier, inc=1, device_id=(peer,), device_id_type=MESH)

    loads = []
    for i, (src, dst) in enumerate(
        ((x_hbm, x_v), (gain_hbm, gain_v), (gate_hbm, gate_v), (up_hbm, up_v), (down_hbm, down_v))
    ):
        cp = pltpu.make_async_copy(src, dst, lsem.at[i])
        cp.start()
        loads.append(cp)
    kloads = []
    for i, src in enumerate((kg_hbm, ku_hbm, kd_hbm)):
        cp = pltpu.make_async_copy(src, k_v.at[i], ksem.at[i])
        cp.start()
        kloads.append(cp)

    loads[0].wait()
    loads[1].wait()
    flat = x_v[...].astype(F32)
    for d in range(R):
        x32[d : d + 1, :] = flat[:, d * 128 : (d + 1) * 128]
    wide = x32[...]
    square = jnp.sum(jnp.sum(wide * wide, axis=1, keepdims=True), axis=0, keepdims=True)
    normed_own = wide * lax.rsqrt(square * (1.0 / D) + 1e-06) * gain_v[...].astype(F32)
    rowbuf[0, a] = normed_own.astype(BF16)

    gacc[...] = jnp.zeros_like(gacc)

    def gram(part, low, high):
        def chunk(i, carry):
            cols = pl.ds(pl.multiple_of(i * 128, 128), 128)
            ks = [k_v[part, j, :, cols].astype(F32) for j in range(BASIS)]
            n = 0
            for i1 in range(BASIS):
                for j1 in range(i1, BASIS):
                    gacc[n] += fold(ks[i1] * ks[j1])
                    n += 1
            return carry

        lax.fori_loop(low, high, chunk, 0)

    pl.semaphore_wait(barrier, len(peers))

    zcps = {}
    for k in NEAR[1:]:
        g = SLOT[Z - k]
        zcps[g] = send(rowbuf.at[0, a], rowbuf.at[g, a], s1.at[g], r1.at[g], dev_z(k))
    o = Z

    def sem1(group, n):
        return o + group * n

    base = Z
    acps = [None, None]
    for h in range(2):
        for g in range(max(1, h * HZ), (h + 1) * HZ):
            zcps[g].wait_recv()
        mine = rowbuf.at[pl.ds(h * HZ, HZ), a]
        acps[h] = []
        for k in range(1, A):
            n = base + h * (A - 1) + k - 1
            acps[h].append(send(mine, mine, s1.at[n], r1.at[n], dev_a(k)))
        if h == 0:
            kloads[0].wait()
            gram(0, 0, R)
    base += 2 * (A - 1)
    bcps = [None, None]
    pcps = [[], []]
    pbase = base + 2 * (A - 1)
    for h in range(2):
        for cp in acps[h]:
            cp.wait_recv()
        for i in range(HZ):
            for j in range(A):
                rows32[pl.ds((i * A + j) * R, R), :] = rowbuf[h * HZ + i, j].astype(F32)
        for d in range(R):
            tok[h, c, b, :, pl.ds(d * 128, 128)] = rows32[pl.ds(d, HZ * A, stride=R), :].astype(BF16)
        mine = tok.at[h, c, b]
        bcps[h] = []
        for k in range(1, A):
            n = base + h * (A - 1) + k - 1
            bcps[h].append(send(mine, mine, s1.at[n], r1.at[n], dev_b(k)))
        n = pbase + h * A
        pcps[h].append(send(mine, mine, s1.at[n], r1.at[n], partner))
    kloads[1].wait()
    loads[2].wait()
    loads[3].wait()
    loads[4].wait()

    def stack(i, carry):
        cols = pl.ds(pl.multiple_of(i * CH, CH), CH)
        parts = [gate_v[:, cols], up_v[:, cols], k_v[0, BASIS - 1, :, cols], k_v[1, BASIS - 1, :, cols]]
        w4t[cols, :] = jnp.concatenate([p.astype(F32) for p in parts], axis=0).T.astype(BF16)
        downt[cols, :] = down_v[:, cols].astype(F32).T.astype(BF16)
        return carry

    lax.fori_loop(0, D // CH, stack, 0)
    len0 = len_ref[0]
    len1 = len_ref[1]
    col = lax.broadcasted_iota(jnp.int32, (L, T), 1)
    row = lax.broadcasted_iota(jnp.int32, (L, T), 0)

    def offset(g):
        k = jnp.zeros_like(g)
        for slot in range(1, Z):
            k = jnp.where(g == slot, NEAR[slot], k)
        return lax.rem(k + z, Z)

    gh = col // (T // 2)
    gc = lax.rem(col // (T // 4), 2)
    gb = lax.rem(col // (HZ * A), A)
    gz = offset(gh * HZ + lax.rem(col // A, HZ))
    ga = lax.rem(col, A)
    gx = ga + gc * (gb - ga)
    gy = gb + gc * (ga - gb)
    token = gz * plane + gx * (2 * A) + gy * 2 + gc
    second = token >= LEN
    inner = jnp.where(second, token - LEN, token)
    live = inner < jnp.where(second, len1, len0)
    place = jnp.where(live, inner + jnp.where(second, len0, 0), -1)
    wanted = offset(row // RZ) * RZ + lax.rem(row, RZ)
    sel[...] = jnp.where(place == wanted, 1.0, 0.0).astype(BF16)
    for h in range(2):
        for k in range(1, A):
            bcps[h][k - 1].wait_recv()
            ref = tok.at[h, c, back_of(b, k, A)]
            n = pbase + h * A + k
            pcps[h].append(send(ref, ref, s1.at[n], r1.at[n], partner))

    every[...] = jnp.zeros_like(every)
    for h in range(2):
        for cp in pcps[h]:
            cp.wait_recv()

        def first(i, carry, h=h):
            cols = pl.ds(pl.multiple_of(i * CW, CW), CW)
            half = tok[h, :, :, :, cols].reshape(T // 2, CW)
            every[h] += mm(half, w4t[cols, :])
            return carry

        lax.fori_loop(0, D // CW, first, 0, unroll=True)
    whole = jnp.concatenate([every[0], every[1]], axis=0)
    moved = None
    for _ in range(3):
        term = whole.astype(BF16)
        whole = whole - term.astype(F32)
        term = mm(sel[...], term)
        moved = term if moved is None else moved + term
    pre[...] = moved.T
    gate_pre = pre[0:F]
    up_pre = pre[F : 2 * F]
    tan_gate = pre[2 * F : 3 * F] * inv_d
    tan_up = pre[3 * F : 4 * F] * inv_d
    act, slope = gelu_pair(gate_pre)
    hidden = act * up_pre
    tangent = slope * tan_gate * up_pre + act * tan_up
    act_v[...] = act
    bend_v[...] = up_pre * slope
    hid_v[...] = hidden.astype(BF16)
    hid_t = hidden.T.astype(BF16)
    tan_t = tangent.T.astype(BF16)
    kloads[2].wait()

    def jvp_block(start):
        cols = pl.ds(pl.multiple_of(start, 128), W)
        return mm(tan_t, down_v[:, cols]) + mm(hid_t, k_v[2, BASIS - 1, :, cols]) * inv_ff

    order = list(range(1, A)) + [0]
    pcps = [None] * A
    for k in order:
        psend[k] = jvp_block((1 - c) * H + step(b, k, A) * W).astype(BF16)
        pcps[k] = send(psend.at[k], precv.at[k], s2.at[k], r2.at[k], partner)
    base = A
    halves = (1, 0)
    acps = [[], []]

    def pass_a(h, k, total):
        if k:
            n = base + h * (A - 1) + k - 1
            asend[h, k - 1] = total.astype(BF16)
            acps[h].append(send(asend.at[h, k - 1], arecv.at[h, k - 1], s2.at[n], r2.at[n], dev_a(k)))
        else:
            own[0, h * HL : (h + 1) * HL, :] = total

    for k in order:
        mine = jvp_block(c * H + step(a, k, A) * W)
        pcps[k].wait_recv()
        total = mine + precv[k].astype(F32)
        own[k] = total
        pass_a(1, k, total[HL:L])
    for k in order:
        pass_a(0, k, own[k, 0:HL, :])
    gram(1, 0, R)
    base += 2 * (A - 1)
    bcps = [[], []]
    for h in halves:
        rows = slice(h * HL, (h + 1) * HL)
        for cp in acps[h]:
            cp.wait_recv()
        for k in order:
            cols = pl.ds(pl.multiple_of(step(b, k, A) * 128, 128), 128)
            total = own[0, rows, cols]
            for j in range(A - 1):
                total = total + arecv[h, j, :, cols].astype(F32)
            if k:
                n = base + h * (A - 1) + k - 1
                bsend[h, k - 1] = total.astype(BF16)
                bcps[h].append(send(bsend.at[h, k - 1], brecv.at[h, k - 1], s2.at[n], r2.at[n], dev_b(k)))
            else:
                zsum[rows, :] = total
    base += 2 * (A - 1)
    zcps = []
    for h in halves:
        rows = slice(h * HL, (h + 1) * HL)
        for cp in bcps[h]:
            cp.wait_recv()
        total = zsum[rows, :]
        for j in range(A - 1):
            total = total + brecv[h, j].astype(F32)
        zsum[rows, :] = total
        for g in range(max(1, h * HZ), (h + 1) * HZ):
            k = NEAR[g]
            start = (g - h * HZ) * RZ
            zsend[g] = total[start : start + RZ].astype(BF16)
            zcps.append(send(zsend.at[g], zrecv.at[k - 1], s2.at[base + k], r2.at[base + k], dev_z(k)))
    def keep(i, carry):
        cols = pl.ds(pl.multiple_of(i * CH, CH), CH)
        nc[:, cols] = mm(sel[...], tok[:, :, :, :, cols].reshape(T, CH)).astype(BF16)
        return carry

    lax.fori_loop(0, D // CH, keep, 0)
    for cp in zcps:
        cp.wait_recv()
    total = zsum[0:RZ, :]
    for j in range(Z - 1):
        total = total + zrecv[j].astype(F32)
    lz[0] = total.astype(BF16)

    zcps = {}
    for k in NEAR[1:]:
        g = SLOT[Z - k]
        zcps[g] = send(lz.at[0], lz.at[g], s3.at[g], r3.at[g], dev_z(k))
    base = Z
    abase = base + NS * (A - 1)
    pbase = abase + NS * 2 * (A - 1)
    bcps = [[] for _ in range(NS)]
    acps = [[] for _ in range(NS)]
    pcps = []

    def build(h):
        for g in range(max(1, h * G), (h + 1) * G):
            zcps[g].wait_recv()
        groups = [lz[g].astype(F32) for g in range(h * G, (h + 1) * G)]
        mine = groups[0] if len(groups) == 1 else jnp.concatenate(groups, axis=0)
        loss[h, c, 0, 0] = mine.astype(BF16)
        ref = loss.at[h, c, 0, 0]
        for k in range(1, A):
            n = base + h * (A - 1) + k - 1
            bcps[h].append(send(ref, loss.at[h, c, 0, k], s3.at[n], r3.at[n], dev_b(k)))
        for k in range(1, A):
            n = abase + h * 2 * (A - 1) + k - 1
            acps[h].append(send(ref, loss.at[h, c, k, 0], s3.at[n], r3.at[n], dev_a(k)))

    def spread(h):
        for cp in bcps[h]:
            cp.wait_recv()
        rest = pl.ds(1, A - 1)
        for k in range(1, A):
            n = abase + (h * 2 + 1) * (A - 1) + k - 1
            acps[h].append(
                send(loss.at[h, c, 0, rest], loss.at[h, c, k, rest], s3.at[n], r3.at[n], dev_a(k))
            )
        ref = loss.at[h, c, 0]
        n = pbase + h * A
        pcps.append(send(ref, ref, s3.at[n], r3.at[n], partner))

    gram(2, 0, R // 2)
    build(0)
    gram(2, R // 2, R)
    qrows[...] = jnp.zeros_like(qrows)
    drows[...] = jnp.zeros_like(drows)
    n = 0
    for i1 in range(BASIS):
        for j1 in range(i1, BASIS):
            q = GRAM + i1 * BASIS + j1
            qrows[q : q + 1, :] = jnp.sum(gacc[n], axis=0, keepdims=True)
            n += 1

    def to_lanes(rows):
        line = jnp.sum(rows[...], axis=1, keepdims=True) * inv_count
        shape = rows.shape
        rowi = lax.broadcasted_iota(jnp.int32, shape, 0)
        coli = lax.broadcasted_iota(jnp.int32, shape, 1)
        return jnp.sum(jnp.where(rowi == coli, line, 0.0), axis=0, keepdims=True)

    gram_tile = to_lanes(qrows)
    for h in range(1, NS):
        build(h)
    for h in range(NS):
        spread(h)
    for h in range(NS):
        for k in range(1, A):
            acps[h][k - 1].wait_recv()
            acps[h][A - 1 + k - 1].wait_recv()
            ref = loss.at[h, c, k]
            n = pbase + h * A + k
            pcps.append(send(ref, ref, s3.at[n], r3.at[n], partner))

    backacc[...] = jnp.zeros_like(backacc)

    def loss_cols(i, width):
        bands = []
        for h in range(NS):
            blocks = []
            for j in range(width // 128):
                n = i * (width // 128) + j
                side = n // (A * A)
                other = side + c - 2 * side * c
                ka = lax.rem(a + other * (b - a) + A - lax.rem(n // A, A), A)
                kb = lax.rem(b + other * (a - b) + A - lax.rem(n, A), A)
                blocks.append(loss[h, side, ka, kb])
            bands.append(jnp.concatenate(blocks, axis=1))
        return jnp.concatenate(bands, axis=0)

    def second_pass(i, carry):
        cols = pl.ds(pl.multiple_of(i * CW, CW), CW)
        backacc[...] += mm(loss_cols(i, CW), downt[cols, :])
        return carry

    def dots(part, grad, i, carry):
        carry = list(carry)
        w_v[part, :, pl.ds(pl.multiple_of(i * CH, CH), CH)] = grad
        for sub in range(CH // 128):
            g = grad[:, sub * 128 : (sub + 1) * 128]
            scols = pl.ds(pl.multiple_of(i * CH + sub * 128, 128), 128)
            for j in range(BASIS):
                carry[j] = carry[j] + fold(k_v[part, j, :, scols].astype(F32) * g)
            carry[BASIS] = carry[BASIS] + fold(g * g)
        return tuple(carry)

    def third(i, carry):
        return dots(2, mm(hid_v[...], loss_cols(i, CH)) * inv_ff, i, carry)

    zero = jnp.zeros((8, 128), F32)
    count = D // CW // 2
    for i in range(count):
        second_pass(c * count + i, 0)
    for cp in pcps:
        cp.wait_recv()
    for i in range(count):
        second_pass((1 - c) * count + i, 0)
    back = backacc[...].T
    both = jnp.concatenate([back * bend_v[...], back * act_v[...]], axis=0).astype(BF16)

    def grads(i, carry):
        cols = pl.ds(pl.multiple_of(i * CH, CH), CH)
        two = mm(both, nc[:, cols]) * inv_d
        return third(i, dots(1, two[F : 2 * F], i, dots(0, two[0:F], i, carry)))

    sums = lax.fori_loop(0, D // CH, grads, (zero,) * (BASIS + 1), unroll=2)
    for j in range(BASIS + 1):
        drows[j : j + 1, :] = jnp.sum(sums[j], axis=0, keepdims=True)
    tile = gram_tile + to_lanes(drows)

    def share(slots, value, at, devs, base):
        slots[at] = value
        cps = []
        for n, dev in enumerate(devs):
            cps.append(send(slots.at[at], slots.at[at], s4.at[base + n], r4.at[base + n], dev))
        for cp in cps:
            cp.wait_recv()
        total = slots[0]
        for j in range(1, len(devs) + 1):
            total = total + slots[j]
        return total

    tile = share(sc_zc, tile, z * 2 + c, [dev_zc(k, flip) for k, flip in zc_group], 0)
    tile = share(sc_xy, tile, x * A + y, [dev_xy(kx, ky) for kx, ky in xy_group], len(zc_group))
    coef_ref[...] = tile
    for cp in pending:
        cp.wait_send()


def finish(cfg, coef_in, w_v, k_v, og_hbm, ou_hbm, od_hbm, coef_ref, out_v, osem):
    D, F, BASIS = cfg
    tile = coef_in[...]
    lane = lax.broadcasted_iota(jnp.int32, (1, 128), 1)
    proj = [
        jnp.sum(jnp.where(lane == j, tile, 0.0), axis=1, keepdims=True) for j in range(BASIS)
    ]
    gi = (lane - GRAM) // BASIS
    gj = lax.rem(lane + (8 * BASIS - GRAM), BASIS)
    left = jnp.zeros_like(tile)
    right = jnp.zeros_like(tile)
    for j in range(BASIS):
        left = left + jnp.where(gi == j, proj[j], 0.0)
        right = right + jnp.where(gj == j, proj[j], 0.0)
    inside = (lane >= GRAM) & (lane < GRAM + BASIS * BASIS)
    weight = jnp.where(inside, jnp.where(gi == gj, 1.0, 2.0), 0.0)
    terms = left * right * tile * weight
    terms = terms + jnp.where(lane == BASIS, tile, 0.0)
    terms = terms - jnp.where(lane < BASIS, 2.0 * tile * tile, 0.0)
    squares = jnp.maximum(jnp.sum(terms, axis=1, keepdims=True), 0.0)
    norm = jnp.sqrt(squares + 1e-06)
    inv_norm = 1.0 / norm
    for j in range(BASIS):
        coef_ref[j] = jnp.sum(jnp.where(lane == j, tile, 0.0))
    coef_ref[BASIS] = jnp.sum(jnp.where(lane == 0, norm, 0.0))

    outs = []
    for part, dst in enumerate((og_hbm, ou_hbm, od_hbm)):

        def final(i, carry, part=part):
            cols = pl.ds(pl.multiple_of(i * 256, 256), 256)
            left_over = w_v[part, :, cols]
            for j in range(BASIS):
                left_over = left_over - proj[j] * k_v[part, j, :, cols].astype(F32)
            out_v[part, :, cols] = (left_over * inv_norm).astype(BF16)
            return carry

        lax.fori_loop(0, D // 256, final, 0, unroll=2)
        cp = pltpu.make_async_copy(out_v.at[part], dst, osem.at[part])
        cp.start()
        outs.append(cp)
    for cp in outs:
        cp.wait()


def per_device(
    inputs, norm_gain, lengths, gate_rows, up_rows, down_rows, krylov_gate, krylov_up, krylov_down
):
    devices = lax.axis_size("fsdp")
    Z, A = sides(devices)
    D = inputs.shape[1]
    T = inputs.shape[0] * devices
    L = T * 3 // 4
    BASIS, F, _ = krylov_gate.shape
    R = D // 128
    H = D // 2
    W = H // A
    HZ = Z // 2
    HL = L // 2
    NS = min(2, Z)
    cfg = (Z, A, D, T, L, F, BASIS)
    pairs = BASIS * (BASIS + 1) // 2
    n1 = Z + 4 * (A - 1) + 2 * A
    n2 = A + 4 * (A - 1) + Z
    n3 = Z + NS * (A - 1) + NS * 2 * (A - 1) + NS * A
    n4 = 2 * Z - 1 + A * A - 1
    hbm = pl.BlockSpec(memory_space=pltpu.HBM)
    vmem = pl.BlockSpec(memory_space=pltpu.VMEM)
    dma = pltpu.SemaphoreType.DMA
    w, k, sums = pl.pallas_call(
        functools.partial(body, cfg),
        out_shape=(
            pltpu.VMEM((3, F, D), F32),
            pltpu.VMEM((3, BASIS, F, D), BF16),
            pltpu.VMEM((1, 128), F32),
        ),
        in_specs=[pl.BlockSpec(memory_space=pltpu.SMEM)] + [hbm] * 8,
        out_specs=(vmem, vmem, vmem),
        scratch_shapes=[
            pltpu.VMEM((1, D), BF16),
            pltpu.VMEM((R, 128), BF16),
            pltpu.VMEM((F, D), BF16),
            pltpu.VMEM((F, D), BF16),
            pltpu.VMEM((F, D), BF16),
            pltpu.VMEM((R, 128), F32),
            pltpu.VMEM((Z, A, R, 128), BF16),
            pltpu.VMEM((HZ * A * R, 128), F32),
            pltpu.VMEM((2, 2, A, HZ * A, D), BF16),
            pltpu.VMEM((D, 4 * F), BF16),
            pltpu.VMEM((D, F), BF16),
            pltpu.VMEM((L, T), BF16),
            pltpu.VMEM((L, D), BF16),
            pltpu.VMEM((2, T // 2, 4 * F), F32),
            pltpu.VMEM((4 * F, L), F32),
            pltpu.VMEM((A, L, W), BF16),
            pltpu.VMEM((A, L, W), BF16),
            pltpu.VMEM((A, L, W), F32),
            pltpu.VMEM((2, A - 1, HL, W), BF16),
            pltpu.VMEM((2, A - 1, HL, W), BF16),
            pltpu.VMEM((2, A - 1, HL, 128), BF16),
            pltpu.VMEM((2, A - 1, HL, 128), BF16),
            pltpu.VMEM((L, 128), F32),
            pltpu.VMEM((Z, L // Z, 128), BF16),
            pltpu.VMEM((Z - 1, L // Z, 128), BF16),
            pltpu.VMEM((Z, L // Z, 128), BF16),
            pltpu.VMEM((NS, 2, A, A, L // NS, 128), BF16),
            pltpu.VMEM((L, F), F32),
            pltpu.VMEM((pairs, 8, 128), F32),
            pltpu.VMEM((128, 128), F32),
            pltpu.VMEM((16, 128), F32),
            pltpu.VMEM((F, L), F32),
            pltpu.VMEM((F, L), F32),
            pltpu.VMEM((F, L), BF16),
            pltpu.VMEM((2 * Z, 1, 128), F32),
            pltpu.VMEM((A * A, 1, 128), F32),
            dma((5,)),
            dma((3,)),
            dma((n1,)),
            dma((n1,)),
            dma((n2,)),
            dma((n2,)),
            dma((n3,)),
            dma((n3,)),
            dma((n4,)),
            dma((n4,)),
        ],
        compiler_params=pltpu.CompilerParams(
            collective_id=0, has_side_effects=True, vmem_limit_bytes=57200000
        ),
        name="arnoldi_step",
    )(
        lengths,
        inputs,
        norm_gain.reshape(R, 128),
        gate_rows,
        up_rows,
        down_rows,
        krylov_gate,
        krylov_up,
        krylov_down,
    )
    part = jax.ShapeDtypeStruct((F, D), BF16)
    return pl.pallas_call(
        functools.partial(finish, (D, F, BASIS)),
        out_shape=(part, part, part, jax.ShapeDtypeStruct((BASIS + 1,), F32)),
        in_specs=[vmem, vmem, vmem],
        out_specs=(hbm, hbm, hbm, pl.BlockSpec(memory_space=pltpu.SMEM)),
        scratch_shapes=[pltpu.VMEM((3, F, D), BF16), dma((3,))],
        compiler_params=pltpu.CompilerParams(vmem_limit_bytes=8 << 20),
        name="arnoldi_finish",
    )(sums, w, k)


def solution(mesh):
    placed = (
        P("fsdp", None),
        P(),
        P(),
        P("fsdp", None),
        P("fsdp", None),
        P("fsdp", None),
        P(None, "fsdp", None),
        P(None, "fsdp", None),
        P(None, "fsdp", None),
    )
    return jax.shard_map(
        per_device,
        mesh=mesh,
        in_specs=placed,
        out_specs=(P("fsdp", None), P("fsdp", None), P("fsdp", None), P()),
        check_vma=False,
    )
```
